32 devices in a mesh: section: 2 (over x), tp: 4 (over z), dp: 4 (over y, core).
Axes of the slice: x: 2, y: 2, z: 4, core: 2. Of those that a mesh axis runs over, the one named last changes fastest.
Arguments:
- stream: bfloat16 [2, 16, 32, 4096], P('section', 'dp', None, 'tp'), may hold values from -120 to 120
- memory_hidden: bfloat16 [16, 32, 4096], P('dp', 'section', 'tp'), may hold values from -120 to 120
- layer_gain: float32 [2, 4096], P('section'), may hold values from 0.5 to 4
- final_gain: float32 [4096], replicated, may hold values from 0.5 to 4
- query_weight: bfloat16 [2, 4096, 4096], P('section', 'dp', 'tp'), may hold values from -0.09375 to 0.09375
- key_weight: bfloat16 [2, 4096, 4096], P('section', 'dp', 'tp'), may hold values from -0.09375 to 0.09375
- value_weight: bfloat16 [2, 4096, 4096], P('section', 'dp', 'tp'), may hold values from -0.09375 to 0.09375
- cotangent: bfloat16 [2, 16, 32, 4096], P('section', 'dp', None, 'tp'), may hold values from -6 to 6
- encoder_lengths: int32 [16], P('dp'), may hold values from 8 to 32
- decoder_lengths: int32 [16], P('dp'), may hold values from 8 to 32
- assignment: int32 [4, 4], P('dp'), may hold values from 0 to 3, each once within a row
Outputs:
- attention_mix: bfloat16 [2, 16, 32, 4096], P('section', 'dp', None, 'tp')
- stream_grad: bfloat16 [2, 16, 32, 4096], P('section', 'dp', None, 'tp')
- memory_grad: bfloat16 [16, 32, 4096], P('dp', 'section', 'tp')
- query_weight_grad: bfloat16 [2, 4096, 4096], P('section', 'dp', 'tp')
- key_weight_grad: bfloat16 [2, 4096, 4096], P('section', 'dp', 'tp')
- value_weight_grad: bfloat16 [2, 4096, 4096], P('section', 'dp', 'tp')
The draws below stay inside these ranges and needn't reach their ends.
Inputs may be any that keep to these rules, and one draw needn't show every extreme that they name: Each row of assignment is a permutation of 0 to 3.
All inputs are finite; a program needn't handle non-finite values.
Results may differ from the reference program's by a relative error of at most 0.019.
The reference program's roundings to bfloat16 on the way count: a program that leaves them out, or rounds other values in their place, can miss the bound.
Values may be sent and summed in bfloat16 or wider, within the bound.
No kernel may reach another device: no remote copies, remote signals or barrier semaphores. Data moves between devices by JAX's collectives and lax.ppermute only.
A program may use at most 128 MiB of HBM per device.

```python
import math
import jax
import jax.numpy as jnp
from jax import lax

D = 4096
HEADS = 64
HEAD_DIM = 64
SEQ = 32
MICRO = 4
SAMPLES = 16
N_SECTION = 2
N_TP = 4
N_DP = 4


def scaled_field(key, extent, rising):
    subkeys = jax.random.split(key, 3)
    row_scale = jnp.exp(jax.random.uniform(subkeys[1], extent[:-1] + (1,), jnp.float32, 0.0, math.log(10.0)))
    if rising:
        position = jnp.arange(extent[-1], dtype=jnp.float32) / (extent[-1] - 1)
        upper = math.log(0.75)
        column_scale = jnp.exp(jax.random.uniform(subkeys[2], (extent[-1],), jnp.float32, math.log(0.3), upper) + math.log(10.0) * position)
        column_scale = jnp.minimum(column_scale, 3.0)
    else:
        column_scale = jnp.exp(jax.random.uniform(subkeys[2], (extent[-1],), jnp.float32, math.log(0.3), math.log(3.0)))
    baseline = jnp.clip(jax.random.normal(subkeys[0], extent, jnp.float32), -4.0, 4.0)
    return (baseline * row_scale * column_scale).astype(jnp.bfloat16)


def gain_field(key, extent, rising):
    lowest, highest = (math.log(0.5), math.log(2.0))
    if rising:
        position = jnp.arange(extent[-1], dtype=jnp.float32) / (extent[-1] - 1)
        base = jax.random.uniform(key, extent, jnp.float32, lowest, highest - math.log(2.0))
        return jnp.exp(base + math.log(2.0) * position)
    return jnp.exp(jax.random.uniform(key, extent, jnp.float32, lowest, highest))


def draw_stream(key, part):
    return scaled_field(jax.random.fold_in(key, 11), (N_SECTION, SAMPLES, SEQ, D), False)


def draw_memory_hidden(key, part):
    return scaled_field(jax.random.fold_in(key, 12), (SAMPLES, SEQ, D), True)


def draw_layer_gain(key, part):
    return gain_field(jax.random.fold_in(key, 13), (N_SECTION, D), False)


def draw_final_gain(key, part):
    return gain_field(jax.random.fold_in(key, 14), (D,), True)


def touch_ends(result, rng, smallest, largest):
    longest = result.shape.index(max(result.shape))
    spots = []
    for shift in (0, 1):
        where = [jax.random.randint(jax.random.fold_in(rng, axis), (), 0, length) for axis, length in enumerate(result.shape)]
        where[longest] = (where[longest] + shift) % result.shape[longest]
        spots.append(tuple(where))
    return result.at[spots[0]].set(smallest).at[spots[1]].set(largest)


def block_levels(own_key, dims, pieces, low, largest):
    level, own = 1.0, jax.random.fold_in(own_key, 6)
    for dim, shards_of in pieces:
        steps = jnp.exp(jax.random.uniform(jax.random.fold_in(own, dim), (shards_of,), jnp.float32, low / len(pieces), largest / len(pieces)))
        level = level * jnp.repeat(steps, dims[dim] // shards_of).reshape([-1 if axis == dim else 1 for axis in range(len(dims))])
    return level


def scatter_about(rng, shape, spread, limit, cuts=(), held_as=jnp.bfloat16):
    result = jax.random.normal(rng, shape, jnp.float32) * spread
    if len(cuts) > 0:
        result = block_levels(rng, shape, cuts, -0.22, 0.18) * result
    return jnp.clip(result, min=-limit, max=limit).astype(held_as)


def setup_inputs(seed: int = 0) -> dict:
    streams_of = jax.random.split(jax.random.key(seed), 12)
    return {
        "stream": draw_stream(jax.random.fold_in(streams_of[11], 71), 0),
        "memory_hidden": draw_memory_hidden(jax.random.fold_in(streams_of[11], 71), 0),
        "layer_gain": draw_layer_gain(jax.random.fold_in(streams_of[11], 71), 0),
        "final_gain": draw_final_gain(jax.random.fold_in(streams_of[11], 71), 0),
        "query_weight": scatter_about(streams_of[4], (N_SECTION, D, HEADS * HEAD_DIM), D ** -0.5, 0.09375, ((0, 2), (1, 4), (2, 4))),
        "key_weight": scatter_about(streams_of[5], (N_SECTION, D, HEADS * HEAD_DIM), D ** -0.5, 0.09375, ((0, 2), (1, 4), (2, 4))),
        "value_weight": scatter_about(streams_of[6], (N_SECTION, D, HEADS * HEAD_DIM), D ** -0.5, 0.09375, ((0, 2), (1, 4), (2, 4))),
        "cotangent": scatter_about(streams_of[7], (N_SECTION, SAMPLES, SEQ, HEADS * HEAD_DIM), 1.0, 6.0, ((0, 2), (1, 4), (3, 4))),
        "encoder_lengths": touch_ends(jax.random.randint(streams_of[8], (SAMPLES,), SEQ // 4, SEQ + 1), jax.random.fold_in(streams_of[8], 1), SEQ // 4, SEQ).astype(jnp.int32),
        "decoder_lengths": touch_ends(jax.random.randint(streams_of[9], (SAMPLES,), SEQ // 4, SEQ + 1), jax.random.fold_in(streams_of[9], 1), SEQ // 4, SEQ).astype(jnp.int32),
        "assignment": jax.vmap(lambda own: jax.random.permutation(own, MICRO))(jax.random.split(streams_of[10], N_DP)).reshape((N_DP, MICRO)).astype(jnp.int32),
    }


EPSILON = 1e-06

def rounded(array):
    return lax.optimization_barrier(array.astype(jnp.bfloat16)).astype(jnp.float32)

def normalize(hidden_in, gain):
    floats = hidden_in.astype(jnp.float32)
    inverse = lax.rsqrt(lax.optimization_barrier(jnp.mean(floats * floats, axis=-1, keepdims=True)) + EPSILON)
    return (floats, inverse, (floats * inverse * gain).astype(jnp.bfloat16))

def norm_backward(floats, inverse, gain, upstream):
    mean_dot = lax.optimization_barrier(jnp.mean(floats * gain * upstream, axis=-1, keepdims=True))
    return inverse * (gain * upstream - floats * (inverse * inverse) * mean_dot)

def attention_core(queries, keys, values, raw_upstream, query_len, key_len):
    span = queries.shape[1]
    score_scale = queries.shape[3] ** (-0.5)
    positions = jnp.arange(span, dtype=jnp.int32)
    key_live = positions[None, :] < key_len[:, None]
    row_live = (positions[None, :] < query_len[:, None]).astype(jnp.float32)[:, :, None, None]
    query_f = queries.astype(jnp.float32)
    key_f = keys.astype(jnp.float32)
    value_f = values.astype(jnp.float32)
    scores = jnp.einsum('bqhe,bkhe->bhqk', query_f, key_f) * score_scale
    scores = jnp.where(key_live[:, None, None, :], scores, -1e+30)
    weights = jax.nn.softmax(scores, axis=-1)
    probs_f = rounded(weights)
    mixture = (jnp.einsum('bhqk,bkhe->bqhe', probs_f, value_f) * row_live).astype(jnp.bfloat16)
    upstream_f = rounded(raw_upstream.astype(jnp.float32) * row_live)
    grad_values = jnp.einsum('bhqk,bqhe->bkhe', probs_f, upstream_f).astype(jnp.bfloat16)
    grad_weights = jnp.einsum('bqhe,bkhe->bhqk', upstream_f, value_f)
    grad_scores = rounded(weights * (grad_weights - lax.optimization_barrier(jnp.sum(grad_weights * weights, axis=-1, keepdims=True))) * score_scale)
    grad_queries = jnp.einsum('bhqk,bkhe->bqhe', grad_scores, key_f).astype(jnp.bfloat16)
    grad_keys = jnp.einsum('bhqk,bqhe->bkhe', grad_scores, query_f).astype(jnp.bfloat16)
    return (mixture, grad_queries, grad_keys, grad_values)

def reference(stream, memory_hidden, layer_gain, final_gain, query_weight, key_weight, value_weight, cotangent, encoder_lengths, decoder_lengths, assignment):
    encoder_count = N_SECTION // 2
    width = HEADS * HEAD_DIM
    group_width = width // N_TP
    token_count = SAMPLES * SEQ
    memory_floats, memory_inverse, memory = normalize(memory_hidden, final_gain)
    chosen = (jnp.arange(N_DP, dtype=jnp.int32)[:, None] * MICRO + assignment).reshape(-1).astype(jnp.int32)
    memory_chosen = memory[chosen]
    decoder_keys = encoder_lengths[chosen]
    memory_accum = jnp.zeros((SAMPLES, SEQ, D), jnp.float32)
    mixtures, stream_grads, query_grads, key_grads, value_grads = ([], [], [], [], [])
    four_dims = (SAMPLES, SEQ, HEADS, HEAD_DIM)
    for layer_index in range(N_SECTION):
        decoder = layer_index >= encoder_count
        floats, inverse, normed = normalize(stream[layer_index], layer_gain[layer_index])
        source = memory_chosen if decoder else normed
        query_len = decoder_lengths if decoder else encoder_lengths
        key_len = decoder_keys if decoder else encoder_lengths
        flat_normed = normed.reshape(token_count, D)
        flat_source = source.reshape(token_count, D)
        queries = jnp.dot(flat_normed, query_weight[layer_index], preferred_element_type=jnp.float32).astype(jnp.bfloat16)
        keys = jnp.dot(flat_source, key_weight[layer_index], preferred_element_type=jnp.float32).astype(jnp.bfloat16)
        values = jnp.dot(flat_source, value_weight[layer_index], preferred_element_type=jnp.float32).astype(jnp.bfloat16)
        mixture, grad_queries, grad_keys, grad_values = attention_core(queries.reshape(four_dims), keys.reshape(four_dims), values.reshape(four_dims), cotangent[layer_index].reshape(four_dims), query_len, key_len)
        mixtures.append(mixture.reshape(SAMPLES, SEQ, width))
        query_groups = grad_queries.reshape(token_count, N_TP, group_width).astype(jnp.float32)
        key_groups = grad_keys.reshape(token_count, N_TP, group_width).astype(jnp.float32)
        value_groups = grad_values.reshape(token_count, N_TP, group_width).astype(jnp.float32)
        query_table = query_weight[layer_index].astype(jnp.float32).reshape(D, N_TP, group_width)
        key_table = key_weight[layer_index].astype(jnp.float32).reshape(D, N_TP, group_width)
        value_table = value_weight[layer_index].astype(jnp.float32).reshape(D, N_TP, group_width)
        partial_value = jnp.einsum('tgh,dgh->gtd', query_groups, query_table)
        source_part = jnp.einsum('tgh,dgh->gtd', key_groups, key_table) + jnp.einsum('tgh,dgh->gtd', value_groups, value_table)
        if decoder:
            memory_accum = memory_accum + lax.optimization_barrier(jnp.sum(source_part, axis=0)).reshape(SAMPLES, SEQ, D)
        else:
            partial_value = partial_value + source_part
        summed = lax.optimization_barrier(jnp.sum(rounded(partial_value), axis=0)).reshape(SAMPLES, SEQ, D)
        stream_grads.append(norm_backward(floats, inverse, layer_gain[layer_index], summed).astype(jnp.bfloat16))
        query_grads.append(jnp.dot(flat_normed.T, grad_queries.reshape(token_count, width), preferred_element_type=jnp.float32).astype(jnp.bfloat16))
        key_grads.append(jnp.dot(flat_source.T, grad_keys.reshape(token_count, width), preferred_element_type=jnp.float32).astype(jnp.bfloat16))
        value_grads.append(jnp.dot(flat_source.T, grad_values.reshape(token_count, width), preferred_element_type=jnp.float32).astype(jnp.bfloat16))
    sample_grad = jnp.zeros((SAMPLES, SEQ, D), jnp.float32).at[chosen].add(memory_accum)
    memory_out = norm_backward(memory_floats, memory_inverse, final_gain, sample_grad).astype(jnp.bfloat16)
    return (jnp.stack(mixtures), jnp.stack(stream_grads), memory_out, jnp.stack(query_grads), jnp.stack(key_grads), jnp.stack(value_grads))
```

```python
import functools

import jax
import jax.numpy as jnp
from jax import lax
from jax.experimental import pallas as pl
from jax.experimental.pallas import tpu as pltpu
from jax.sharding import PartitionSpec as P

HEAD_DIM = 64
EPSILON = 1e-06
CHUNKS = 2

BF16 = jnp.bfloat16
F32 = jnp.float32


def dot(left, right, over):
    return lax.dot_general(left, right, (over, ((), ())), preferred_element_type=F32)


def attention_kernel(
    own_ref, got_ref, up_ref, scale_q_ref, scale_s_ref, open_ref, live_ref,
    mix_ref, grad_ref, dot_q_ref, dot_s_ref,
):
    score_scale = HEAD_DIM ** (-0.5)
    scale_q, scale_s, live = scale_q_ref[...], scale_s_ref[...], live_ref[...]
    summed = own_ref[...] + got_ref[...].astype(F32)
    q = (summed[0] * scale_q).astype(BF16)
    k = (summed[1] * scale_s).astype(BF16)
    v = (summed[2] * scale_s).astype(BF16)
    up = (up_ref[...].astype(F32) * live).astype(BF16)
    allowed = open_ref[...] > 0.0
    lane = lax.broadcasted_iota(jnp.int32, q.shape, 1)
    mix = gq = gk = gv = None
    for head in range(q.shape[1] // HEAD_DIM):
        mine = (lane // HEAD_DIM) == head
        zero = jnp.zeros_like(q)
        qm, km = jnp.where(mine, q, zero), jnp.where(mine, k, zero)
        vm, um = jnp.where(mine, v, zero), jnp.where(mine, up, zero)
        scores = jnp.where(allowed, dot(qm, k, ((1,), (1,))) * score_scale, -1e30)
        top = jnp.max(scores, axis=-1, keepdims=True)
        powers = jnp.exp(scores - top)
        weights = powers / jnp.sum(powers, axis=-1, keepdims=True)
        probs = weights.astype(BF16)
        grad_weights = dot(um, v, ((1,), (1,)))
        inner = jnp.sum(grad_weights * weights, axis=-1, keepdims=True)
        grad_scores = (weights * (grad_weights - inner) * score_scale).astype(BF16)
        parts = (
            dot(probs, vm, ((1,), (0,))),
            dot(grad_scores, km, ((1,), (0,))),
            dot(grad_scores, qm, ((0,), (0,))),
            dot(probs, um, ((0,), (0,))),
        )
        if mix is None:
            mix, gq, gk, gv = parts
        else:
            mix, gq, gk, gv = mix + parts[0], gq + parts[1], gk + parts[2], gv + parts[3]
    mix_ref[...] = (mix * live).astype(BF16)
    grad_ref[0] = (gq * scale_q).astype(BF16)
    grad_ref[1] = (gk * scale_s).astype(BF16)
    grad_ref[2] = (gv * scale_s).astype(BF16)

    @pl.when(pl.program_id(0) == 0)
    def _():
        dot_q_ref[...] = jnp.zeros_like(dot_q_ref)
        dot_s_ref[...] = jnp.zeros_like(dot_s_ref)

    dot_q_ref[...] += gq * q.astype(F32)
    dot_s_ref[...] += gk * k.astype(F32) + gv * v.astype(F32)


def attention(own, got, upstream, scale_q, scale_s, opened, live, first):
    three, tokens, columns = own.shape
    lanes = min(columns, 2 * HEAD_DIM)
    start = first // lanes
    wide = pl.BlockSpec((three, tokens, lanes), lambda p: (0, 0, p))
    flat = pl.BlockSpec((tokens, lanes), lambda p: (0, p))
    whole = lambda shape: pl.BlockSpec(shape, lambda p: (0, 0))
    return pl.pallas_call(
        attention_kernel,
        grid=(columns // lanes,),
        out_shape=(
            jax.ShapeDtypeStruct((tokens, columns), BF16),
            jax.ShapeDtypeStruct((three, tokens, columns), BF16),
            jax.ShapeDtypeStruct((tokens, lanes), F32),
            jax.ShapeDtypeStruct((tokens, lanes), F32),
        ),
        in_specs=[
            wide, wide, pl.BlockSpec((tokens, lanes), lambda p: (0, p + start)),
            whole((tokens, 1)), whole((tokens, 1)), whole((tokens, tokens)), whole((tokens, 1)),
        ],
        out_specs=(flat, wide, whole((tokens, lanes)), whole((tokens, lanes))),
        cost_estimate=pl.CostEstimate(
            flops=12 * tokens * tokens * columns, bytes_accessed=24 * tokens * columns, transcendentals=0
        ),
        name="attention",
    )(own, got, upstream, scale_q, scale_s, opened, live)


SMEM = pl.BlockSpec(memory_space=pltpu.SMEM)
GRANT = 56 * 1024 * 1024


def full(array):
    return pl.BlockSpec(array.shape, lambda i, n=len(array.shape): (0,) * n)


def shaped(shape, dtype):
    return jax.ShapeDtypeStruct(shape, dtype)


def columns_of(weight, width, c):
    return pl.BlockSpec((weight.shape[0], width), lambda i: (0, c))


def cost(*dots):
    return pl.CostEstimate(flops=2 * sum(dots), bytes_accessed=sum(dots) // 512, transcendentals=0)


def product(left, weight, over):
    return lax.dot_general(left, weight, (over, ((), ())), preferred_element_type=F32)


def multiply(x_ref, s_ref, weight_refs, keep_ref, send_ref):
    places, tokens, rows = x_ref.shape
    half = places // 2
    for i, w_ref in enumerate(weight_refs):
        lhs = x_ref if i == 0 else s_ref
        weight = w_ref[...]
        upper = lhs[half:].reshape(half * tokens, rows)
        send_ref[i] = product(upper, weight, ((1,), (0,))).astype(BF16)
        lower = lhs[:half].reshape(half * tokens, rows)
        keep_ref[i] = product(lower, weight, ((1,), (0,)))


def first_kernel(n_tp, n_sec, share, where_ref, *refs):
    arrived = refs[:n_tp]
    memory = refs[n_tp : n_tp + n_sec]
    weight_refs = refs[n_tp + n_sec : n_tp + n_sec + 3]
    x_ref, s_ref, keep_ref, send_ref = refs[n_tp + n_sec + 3 :]
    places, tokens, rows = x_ref.shape
    part = tokens // n_sec
    sec, decoder = where_ref[2 * n_tp], where_ref[2 * n_tp + 1]
    for j in range(n_tp):
        at = where_ref[j]
        lanes = pl.ds(pl.multiple_of(where_ref[n_tp + j] * share, share), share)
        x_ref[at, :, lanes] = arrived[j][...]

        @pl.when(decoder == 0)
        def _():
            s_ref[at, :, lanes] = arrived[j][...]

        @pl.when(decoder == 1)
        def _():
            for i in range(n_sec):
                first = pl.multiple_of(lax.rem(sec - i + n_sec, n_sec) * part, part)
                s_ref[at, pl.ds(first, part), lanes] = memory[i][j]

    multiply(x_ref, s_ref, weight_refs, keep_ref, send_ref)


def later_kernel(x_ref, s_ref, wq_ref, wk_ref, wv_ref, keep_ref, send_ref):
    multiply(x_ref, s_ref, (wq_ref, wk_ref, wv_ref), keep_ref, send_ref)


def project(c, width, weights, places, n_sec, where, arrived=None, memory=None, x=None, s=None):
    rows = weights[0].shape[0]
    tokens = arrived[0].shape[0] if x is None else x.shape[1]
    half = places * tokens // 2
    weight_specs = [columns_of(w, width, c) for w in weights]
    outs = (shaped((3, half, width), F32), shaped((3, half, width), BF16))
    params = pltpu.CompilerParams(vmem_limit_bytes=GRANT)
    estimate = cost(3 * places * tokens * rows * width)
    if x is None:
        held = shaped((places, tokens, rows), BF16)
        outs = (held, held) + outs
        return pl.pallas_call(
            functools.partial(first_kernel, len(arrived), n_sec, arrived[0].shape[1]),
            grid=(1,),
            in_specs=[SMEM] + [full(a) for a in arrived] + [full(m) for m in memory] + weight_specs,
            out_specs=tuple(full(o) for o in outs),
            out_shape=outs,
            compiler_params=params,
            cost_estimate=estimate,
            name="project_first",
        )(where, *arrived, *memory, *weights)
    return (x, s) + tuple(
        pl.pallas_call(
            later_kernel,
            grid=(1,),
            in_specs=[full(x), full(s)] + weight_specs,
            out_specs=tuple(full(o) for o in outs),
            out_shape=outs,
            compiler_params=params,
            cost_estimate=estimate,
            name="project_later",
        )(x, s, *weights)
    )


def combine_kernel(keep_ref, got_ref, own_ref, send_ref):
    half = own_ref.shape[1]
    own_ref[0] = keep_ref[0, :half] + got_ref[0, :half].astype(F32)
    send_ref[0] = (keep_ref[0, half:] + got_ref[0, half:].astype(F32)).astype(BF16)


def combine(keep, got):
    three, rows, width = keep.shape
    block = lambda n: pl.BlockSpec((1, n, width), lambda i: (i, 0, 0))
    return pl.pallas_call(
        combine_kernel,
        grid=(three,),
        in_specs=[block(rows), block(rows)],
        out_specs=(block(rows // 2), block(rows // 2)),
        out_shape=(shaped((three, rows // 2, width), F32), shaped((three, rows // 2, width), BF16)),
        cost_estimate=pl.CostEstimate(flops=keep.size, bytes_accessed=8 * keep.size, transcendentals=0),
        name="combine",
    )(keep, got)


def back_kernel(n_sec, last, flags_ref, *refs):
    count = len(refs) - (8 + n_sec if last else 5)
    grads, refs = refs[:count], refs[count:]
    weight_refs, refs = refs[:3], refs[3:]
    sec, decoder = flags_ref[0], flags_ref[1]
    tokens = grads[0].shape[1]
    left = [jnp.concatenate([g[i] for g in grads], axis=0) if count > 1 else grads[0][i] for i in range(3)]
    query = product(left[0], weight_refs[0][...], ((1,), (1,)))
    source = product(left[1], weight_refs[1][...], ((1,), (1,)))
    source = source + product(left[2], weight_refs[2][...], ((1,), (1,)))
    stream = query + jnp.where(decoder == 1, 0.0, source)
    memory = jnp.where(decoder == 1, source, 0.0)
    rows = query.shape[1]
    if not last:
        stream_ref, memory_ref = refs
        stream_ref[...] = stream.reshape(stream_ref.shape)
        memory_ref[...] = memory.reshape(memory_ref.shape)
        return
    acc_s, acc_m, part_a, part_b = refs[:4]
    memory_refs, scratch = refs[4:-1], refs[-1]
    part = tokens // 2
    piece = tokens // n_sec
    for p in range(count):
        here = stream[p * tokens : (p + 1) * tokens] + acc_s[p, 0]
        part_a[p] = here[:part].astype(BF16)
        part_b[p] = here[part:].astype(BF16)
        scratch[...] = memory[p * tokens : (p + 1) * tokens] + acc_m[p, 0]
        for i, ref in enumerate(memory_refs):
            first = pl.multiple_of(lax.rem(sec + i, n_sec) * piece, piece)
            ref[p] = scratch[pl.ds(first, piece)].astype(ref.dtype)


def back(c, width, weights, grads, flags, n_sec, acc=None, odd=0):
    tokens, rows, places = grads[0].shape[1], weights[0].shape[0], len(grads)
    weight_specs = [columns_of(w, width, c) for w in weights]
    params = pltpu.CompilerParams(vmem_limit_bytes=GRANT)
    estimate = cost(3 * places * tokens * rows * width)
    if acc is None:
        outs = (shaped((places // 2, 2, tokens, rows), F32),) * 2
        return pl.pallas_call(
            functools.partial(back_kernel, n_sec, False),
            grid=(1,),
            in_specs=[SMEM] + [full(g) for g in grads] + weight_specs,
            out_specs=tuple(full(o) for o in outs),
            out_shape=outs,
            compiler_params=params,
            cost_estimate=estimate,
            name="back_first",
        )(flags, *grads, *weights)
    outs = (shaped((places, tokens // 2, rows), BF16),) * 2
    piece = (places, tokens // n_sec, rows)
    outs += (shaped(piece, F32),) + (shaped(piece, BF16),) * (n_sec - 1)
    acc_spec = pl.BlockSpec((places, 1, tokens, rows), lambda i: (0, odd, 0, 0))
    return pl.pallas_call(
        functools.partial(back_kernel, n_sec, True),
        grid=(1,),
        in_specs=[SMEM] + [full(g) for g in grads] + weight_specs + [acc_spec, acc_spec],
        out_specs=tuple(full(o) for o in outs),
        out_shape=outs,
        scratch_shapes=[pltpu.VMEM((tokens, rows), F32)],
        compiler_params=params,
        cost_estimate=estimate,
        name="back_last",
    )(flags, *grads, *weights, *acc)


def pick_kernel(n_tp, share, pick_ref, own_ref, got_ref, *out_refs):
    for j in range(n_tp):
        at = pick_ref[j, 1]
        lanes = pl.ds(pl.multiple_of(pick_ref[j, 2] * share, share), share)

        @pl.when(pick_ref[j, 0] == 0)
        def _():
            out_refs[j][...] = own_ref[at, :, lanes]

        @pl.when(pick_ref[j, 0] == 1)
        def _():
            out_refs[j][...] = got_ref[at, :, lanes]


def pick(picks, own, got, n_tp, share):
    outs = (shaped((own.shape[1], share), own.dtype),) * n_tp
    return pl.pallas_call(
        functools.partial(pick_kernel, n_tp, share),
        grid=(1,),
        in_specs=[SMEM, full(own), full(got)],
        out_specs=tuple(full(o) for o in outs),
        out_shape=outs,
        cost_estimate=pl.CostEstimate(flops=0, bytes_accessed=4 * own.size, transcendentals=0),
        name="pick",
    )(picks, own, got)


def swap(array, axis, size, bit):
    return lax.ppermute(array, axis, [(i, i ^ bit) for i in range(size)])


def shift(array, by):
    size = lax.axis_size("section")
    return lax.ppermute(array, "section", [(s, (s + by) % size) for s in range(size)])


def sum_over(array, axis):
    size, bit = lax.axis_size(axis), 1
    while bit < size:
        array = array + swap(array, axis, size, bit)
        bit *= 2
    return array


def reversed_bits(index, size):
    result, bit = 0, 1
    while bit < size:
        result = result * 2 + (1 if index & bit else 0)
        bit *= 2
    return result


def shards(
    stream, memory_hidden, layer_gain, final_gain, query_weight, key_weight, value_weight,
    cotangent, encoder_lengths, decoder_lengths, assignment,
):
    n_sec, n_tp, n_dp = (lax.axis_size(a) for a in ("section", "tp", "dp"))
    sec, tp, dp = (lax.axis_index(a) for a in ("section", "tp", "dp"))
    decoder = sec >= n_sec // 2
    local = stream[0]
    micro, span, share = local.shape
    slots = memory_hidden.shape[1]
    hidden = share * n_tp
    columns = query_weight.shape[2]
    tokens, mem_tokens = micro * span, micro * slots
    per_row = n_tp // n_dp
    half = n_dp // 2
    width = columns // CHUNKS
    weights = [w[0] for w in (query_weight, key_weight, value_weight)]

    def to_rows(x):
        return x.reshape(micro, n_sec, slots, -1).transpose(1, 0, 2, 3).reshape(tokens, -1)

    def to_samples(x):
        return x.reshape(n_sec, micro, slots, -1).transpose(1, 0, 2, 3).reshape(micro, span, -1)

    layer_share = lax.dynamic_slice_in_dim(layer_gain[0], tp * share, share)
    final_share = lax.dynamic_slice_in_dim(final_gain, tp * share, share)
    stream_f = local.astype(F32)
    memory_f = memory_hidden.astype(F32)
    stream_block = to_rows((stream_f * layer_share).astype(BF16))
    memory_block = (memory_f * final_share).astype(BF16).reshape(mem_tokens, share)

    inward = []
    for j in range(n_tp):
        pairs = []
        for z in range(n_tp):
            for r in range(n_dp):
                to = ((z % per_row) * n_dp + r + j) % n_tp
                pairs.append((z * n_dp + r, to * n_dp + z // per_row))
        inward.append(pairs)
    with jax.named_scope("in_memory"):
        mem_own = jnp.stack([lax.ppermute(memory_block, ("tp", "dp"), pairs) for pairs in inward])
    with jax.named_scope("in_stream"):
        arrived = [lax.ppermute(stream_block, ("tp", "dp"), pairs) for pairs in inward]
    with jax.named_scope("x_memory"):
        memory = [mem_own] + [shift(mem_own, i) for i in range(1, n_sec)]
    units = [(tp - j) % n_tp for j in range(n_tp)]
    place_of = [reversed_bits(p, n_dp) for p in range(n_dp)]

    def place(index):
        return sum(jnp.where(index == k, place_of[k], 0) for k in range(n_dp))

    where = jnp.stack(
        [place((u % n_dp) ^ dp) for u in units] + [u // n_dp for u in units] + [sec, decoder.astype(jnp.int32)]
    ).astype(jnp.int32)
    flags = jnp.stack([sec, decoder.astype(jnp.int32)]).astype(jnp.int32)

    squares = jnp.concatenate(
        [
            jnp.sum(stream_f * stream_f, axis=2).reshape(micro, n_sec, slots).transpose(1, 0, 2).reshape(tokens),
            jnp.sum(memory_f * memory_f, axis=2).reshape(mem_tokens),
        ]
    )
    inverses = lax.rsqrt(sum_over(squares, "tp") / hidden + EPSILON)
    inverse, mem_inverse = inverses[:tokens], inverses[tokens:]
    scales = [mem_inverse] + [shift(mem_inverse, i) for i in range(1, n_sec)]
    mem_scale = [
        sum(jnp.where((sec - i) % n_sec == h, scales[i], 0.0) for i in range(n_sec)) for h in range(n_sec)
    ]
    scale_q = inverse[:, None]
    scale_s = jnp.where(decoder, jnp.concatenate(mem_scale), inverse)[:, None]

    micros = jnp.arange(micro, dtype=jnp.int32)
    reads = jnp.where(decoder, assignment[0], micros)
    query_len = jnp.where(decoder, decoder_lengths, encoder_lengths)
    index = jnp.arange(tokens, dtype=jnp.int32)
    sample = (index // slots) % micro
    position = (index // (micro * slots)) * slots + index % slots

    def of_sample(values):
        return sum(jnp.where(sample == m, values[m], 0) for m in range(micro))

    opened = (of_sample(reads)[:, None] == sample[None, :]) & (position < of_sample(encoder_lengths))[None, :]
    opened = opened.astype(F32)
    live = (position < of_sample(query_len)).astype(F32)[:, None]
    raw = to_rows(cotangent[0])

    mixes, grads, dot_q, dot_s = [], [], 0.0, 0.0
    x = s = acc = None
    for c in range(CHUNKS):
        if c == 0:
            x, s, keep, send = project(c, width, weights, n_dp, n_sec, where, arrived, memory)
        else:
            x, s, keep, send = project(c, width, weights, n_dp, n_sec, where, x=x, s=s)
        bit = 1
        while True:
            with jax.named_scope(f"reduce_{bit}_{c}"):
                got = swap(send, "dp", n_dp, bit)
            bit *= 2
            if bit == n_dp:
                break
            keep, send = combine(keep, got)
        with jax.named_scope(f"attention_{c}"):
            mix, grad, piece_q, piece_s = attention(
                keep, got, raw, scale_q, scale_s, opened, live, c * width
            )
        mixes.append(mix)
        dot_q, dot_s = dot_q + piece_q, dot_s + piece_s
        held = [grad]
        while bit > 1:
            bit //= 2
            with jax.named_scope(f"gather_{bit}_{c}"):
                held = held + [swap(h, "dp", n_dp, bit) for h in held]
        grads.append(held)
        if c < CHUNKS - 1:
            new = back(c, width, weights, held, flags, n_sec)
            acc = new if acc is None else (acc[0] + new[0], acc[1] + new[1])

    row_q, row_s = jnp.sum(dot_q, axis=1), jnp.sum(dot_s, axis=1)
    row_stream = row_q + jnp.where(decoder, 0.0, row_s)
    row_memory = jnp.where(decoder, row_s, 0.0).reshape(n_sec, mem_tokens)
    mem_rows = lax.dynamic_slice_in_dim(row_memory, sec, 1, 0)
    for i in range(1, n_sec):
        mem_rows = mem_rows + shift(lax.dynamic_slice_in_dim(row_memory, (sec + i) % n_sec, 1, 0), i)
    row_dots = sum_over(jnp.concatenate([row_stream, mem_rows.reshape(mem_tokens)]), "tp") / hidden

    swapped = back(CHUNKS - 1, width, weights, grads[-1][1::2], flags, n_sec, acc, 1)
    kept = back(CHUNKS - 1, width, weights, grads[-1][0::2], flags, n_sec, acc, 0)

    def memory_sum(parts):
        total = parts[2]
        for i in range(1, n_sec):
            total = total + shift(parts[2 + i], i).astype(F32)
        return total.astype(BF16)

    leaving = [(kept[0], swapped[0]), (kept[1], swapped[1]), (memory_sum(kept), memory_sum(swapped))]
    rows_of = [u // per_row % half for u in units]
    picks = jnp.stack(
        [
            jnp.stack(
                [
                    u // (per_row * half),
                    sum(jnp.where(rows_of[j] == b, reversed_bits(b, half), 0) for b in range(half)),
                    u % per_row,
                ]
            )
            for j, u in enumerate(units)
        ]
    ).astype(jnp.int32)
    totals = []
    for part, (own, away) in enumerate(leaving):
        with jax.named_scope(f"turn_{part}"):
            back_here = swap(away, "dp", n_dp, half)
        sent = pick(picks, own, back_here, n_tp, share)
        total = 0.0
        for j in range(n_tp):
            pairs = []
            for z in range(n_tp):
                u = (z - j) % n_tp
                a, b, f = u // (per_row * half), u // per_row % half, u % per_row
                for r in range(n_dp):
                    pairs.append((z * n_dp + r, ((r ^ (a * half)) * per_row + f) * n_dp + (r ^ b)))
            with jax.named_scope(f"out_{part}"):
                total = total + lax.ppermute(sent[j], ("tp", "dp"), pairs).astype(F32)
        totals.append(total)
    total = to_samples(jnp.concatenate(totals[:2], axis=0))
    factor = to_samples(inverse * inverse * row_dots[:tokens])
    stream_out = layer_share * total - stream_f * factor
    mem_factor = (mem_inverse * mem_inverse * row_dots[tokens:]).reshape(micro, slots, 1)
    memory_out = final_share * totals[2].reshape(micro, slots, share) - memory_f * mem_factor

    def weight_grad(left, i):
        rows = [jnp.concatenate([grads[c][p][i] for c in range(CHUNKS)], axis=-1) for p in range(n_dp)]
        return dot(
            left.reshape(n_dp * tokens, -1), jnp.concatenate(rows, axis=0), ((0,), (0,))
        ).astype(BF16)[None]

    return (
        to_samples(jnp.concatenate(mixes, axis=-1))[None],
        stream_out.astype(BF16)[None],
        memory_out.astype(BF16),
        weight_grad(x, 0),
        weight_grad(s, 1),
        weight_grad(s, 2),
    )


def solution(mesh):
    placed = (
        P("section", "dp", None, "tp"),
        P("dp", "section", "tp"),
        P("section", None),
        P(),
        P("section", "dp", "tp"),
        P("section", "dp", "tp"),
        P("section", "dp", "tp"),
        P("section", "dp", None, "tp"),
        P("dp"),
        P("dp"),
        P("dp", None),
    )
    return jax.shard_map(
        shards,
        mesh=mesh,
        in_specs=placed,
        out_specs=(
            P("section", "dp", None, "tp"),
            P("section", "dp", None, "tp"),
            P("dp", "section", "tp"),
            P("section", "dp", "tp"),
            P("section", "dp", "tp"),
            P("section", "dp", "tp"),
        ),
        check_vma=False,
    )
```

```python
import functools

import jax
import jax.numpy as jnp
import numpy as np
from jax import lax
from jax.experimental import pallas as pl
from jax.experimental.pallas import tpu as pltpu
from jax.sharding import PartitionSpec as P

HEAD_DIM = 64
EPSILON = 1e-06
CHUNKS = 2
MIB = 1024 * 1024
PARTS = 1

BF16 = jnp.bfloat16
F32 = jnp.float32


def dot(left, right, over):
    return lax.dot_general(left, right, (over, ((), ())), preferred_element_type=F32)


def attention_kernel(
    own_ref, got_ref, up_ref, scale_q_ref, scale_s_ref, open_ref, live_ref,
    mix_ref, grad_ref, dot_q_ref, dot_s_ref,
):
    score_scale = HEAD_DIM ** (-0.5)
    scale_q, scale_s, live = scale_q_ref[...], scale_s_ref[...], live_ref[...]
    allowed = open_ref[...] > 0.0
    tokens, lanes = dot_q_ref.shape
    lane = lax.broadcasted_iota(jnp.int32, (tokens, lanes), 1)
    dot_q = dot_s = jnp.zeros((tokens, lanes), F32)

    def beside(parts):
        return jnp.concatenate(parts, axis=1)

    def below(parts):
        return jnp.concatenate(parts, axis=0)

    for p in range(own_ref.shape[2] // lanes):
        at = pl.ds(p * lanes, lanes)

        def projected(i, scale):
            return ((own_ref[i, :, at] + got_ref[i, :, at].astype(F32)) * scale).astype(BF16)

        q, k, v = projected(0, scale_q), projected(1, scale_s), projected(2, scale_s)
        up = (up_ref[:, at].astype(F32) * live).astype(BF16)
        zero = jnp.zeros_like(q)
        heads = []
        for head in range(lanes // HEAD_DIM):
            mine = (lane // HEAD_DIM) == head
            qm, km, vm, um = (jnp.where(mine, a, zero) for a in (q, k, v, up))
            scores = jnp.where(allowed, dot(qm, k, ((1,), (1,))) * score_scale, -1e30)
            top = jnp.max(scores, axis=-1, keepdims=True)
            powers = jnp.exp(scores - top)
            weights = powers * (1.0 / jnp.sum(powers, axis=-1, keepdims=True))
            grad_weights = dot(um, v, ((1,), (1,)))
            inner = jnp.sum(grad_weights * weights, axis=-1, keepdims=True)
            grad_scores = (weights * (grad_weights - inner) * score_scale).astype(BF16)
            heads.append((weights.astype(BF16), grad_scores, qm, km, vm, um))
        probs, grad_scores, qs, ks, vs, ups = zip(*heads)
        mix = dot(beside(probs), below(vs), ((1,), (0,)))
        gq = dot(beside(grad_scores), below(ks), ((1,), (0,)))
        gk = dot(below(grad_scores), below(qs), ((0,), (0,)))
        gv = dot(below(probs), below(ups), ((0,), (0,)))
        mix_ref[:, at] = (mix * live).astype(BF16)
        grad_ref[0, :, at] = (gq * scale_q).astype(BF16)
        grad_ref[1, :, at] = (gk * scale_s).astype(BF16)
        grad_ref[2, :, at] = (gv * scale_s).astype(BF16)
        dot_q = dot_q + gq * q.astype(F32)
        dot_s = dot_s + gk * k.astype(F32) + gv * v.astype(F32)
    dot_q_ref[...] = dot_q
    dot_s_ref[...] = dot_s


def attention(own, got, upstream, scale_q, scale_s, opened, live, c):
    three, tokens, columns = own.shape
    lanes = min(columns, 2 * HEAD_DIM)
    outs = (
        shaped((tokens, columns), BF16),
        shaped((three, tokens, columns), BF16),
        shaped((tokens, lanes), F32),
        shaped((tokens, lanes), F32),
    )
    args = (own, got, upstream, scale_q, scale_s, opened, live)
    specs = [full(a) for a in args]
    specs[2] = pl.BlockSpec((tokens, columns), lambda i: (0, c))
    return pl.pallas_call(
        attention_kernel,
        grid=(1,),
        out_shape=outs,
        in_specs=specs,
        out_specs=tuple(full(o) for o in outs),
        compiler_params=pltpu.CompilerParams(vmem_limit_bytes=10 * MIB),
        cost_estimate=pl.CostEstimate(
            flops=2 * 1024 * tokens * tokens * columns // 64, bytes_accessed=24 * tokens * columns, transcendentals=0
        ),
        name="attention",
    )(*args)


SMEM = pl.BlockSpec(memory_space=pltpu.SMEM)


def full(array):
    return pl.BlockSpec(array.shape, lambda i, n=len(array.shape): (0,) * n)


def shaped(shape, dtype):
    return jax.ShapeDtypeStruct(shape, dtype)


def columns_of(weight, width, c):
    return pl.BlockSpec((weight.shape[0], width), lambda i: (0, c))


def cost(*dots):
    return pl.CostEstimate(flops=2 * sum(dots), bytes_accessed=sum(dots) // 512, transcendentals=0)


def product(left, weight, over):
    return lax.dot_general(left, weight, (over, ((), ())), preferred_element_type=F32)


def multiply(x_ref, s_ref, weight_refs, keep_ref, send_ref):
    places, tokens, rows = x_ref.shape
    half = places // 2
    for i, w_ref in enumerate(weight_refs):
        lhs = x_ref if i == 0 else s_ref
        weight = w_ref[...]
        upper = lhs[half:].reshape(half * tokens, rows)
        send_ref[i] = product(upper, weight, ((1,), (0,))).astype(BF16)
        lower = lhs[:half].reshape(half * tokens, rows)
        keep_ref[i] = product(lower, weight, ((1,), (0,)))


def first_kernel(n_tp, n_sec, share, where_ref, *refs):
    arrived = refs[:n_tp]
    memory = refs[n_tp : n_tp + n_sec]
    weight_refs = refs[n_tp + n_sec : n_tp + n_sec + 3]
    x_ref, s_ref, keep_ref, send_ref = refs[n_tp + n_sec + 3 :]
    places, tokens, rows = x_ref.shape
    part = tokens // n_sec
    sec, decoder = where_ref[2 * n_tp], where_ref[2 * n_tp + 1]
    for j in range(n_tp):
        at = where_ref[j]
        lanes = pl.ds(pl.multiple_of(where_ref[n_tp + j] * share, share), share)
        x_ref[at, :, lanes] = arrived[j][...]

        @pl.when(decoder == 0)
        def _():
            s_ref[at, :, lanes] = arrived[j][...]

        @pl.when(decoder == 1)
        def _():
            for i in range(n_sec):
                first = pl.multiple_of(lax.rem(sec - i + n_sec, n_sec) * part, part)
                s_ref[at, pl.ds(first, part), lanes] = memory[i][j]

    multiply(x_ref, s_ref, weight_refs, keep_ref, send_ref)


def later_kernel(x_ref, s_ref, wq_ref, wk_ref, wv_ref, keep_ref, send_ref):
    multiply(x_ref, s_ref, (wq_ref, wk_ref, wv_ref), keep_ref, send_ref)


def project(c, width, weights, places, n_sec, where, arrived=None, memory=None, x=None, s=None):
    rows = weights[0].shape[0]
    tokens = arrived[0].shape[0] if x is None else x.shape[1]
    half = places * tokens // 2
    weight_specs = [columns_of(w, width, c) for w in weights]
    outs = (shaped((3, half, width), F32), shaped((3, half, width), BF16))
    params = pltpu.CompilerParams(vmem_limit_bytes=20 * MIB)
    estimate = cost(3 * places * tokens * rows * width)
    if x is None:
        held = shaped((places, tokens, rows), BF16)
        outs = (held, held) + outs
        return pl.pallas_call(
            functools.partial(first_kernel, len(arrived), n_sec, arrived[0].shape[1]),
            grid=(1,),
            in_specs=[SMEM] + [full(a) for a in arrived] + [full(m) for m in memory] + weight_specs,
            out_specs=tuple(full(o) for o in outs),
            out_shape=outs,
            compiler_params=params,
            cost_estimate=estimate,
            name="project_first",
        )(where, *arrived, *memory, *weights)
    return (x, s) + tuple(
        pl.pallas_call(
            later_kernel,
            grid=(1,),
            in_specs=[full(x), full(s)] + weight_specs,
            out_specs=tuple(full(o) for o in outs),
            out_shape=outs,
            compiler_params=params,
            cost_estimate=estimate,
            name="project_later",
        )(x, s, *weights)
    )


def combine_kernel(keep_ref, got_ref, own_ref, send_ref):
    half = own_ref.shape[1]
    own_ref[...] = keep_ref[:, :half] + got_ref[:, :half].astype(F32)
    send_ref[...] = (keep_ref[:, half:] + got_ref[:, half:].astype(F32)).astype(BF16)


def combine(keep, got):
    three, rows, width = keep.shape
    outs = (shaped((three, rows // 2, width), F32), shaped((three, rows // 2, width), BF16))
    return pl.pallas_call(
        combine_kernel,
        grid=(1,),
        in_specs=[full(keep), full(got)],
        out_specs=tuple(full(o) for o in outs),
        out_shape=outs,
        compiler_params=pltpu.CompilerParams(vmem_limit_bytes=12 * MIB),
        cost_estimate=pl.CostEstimate(flops=keep.size, bytes_accessed=8 * keep.size, transcendentals=0),
        name="combine",
    )(keep, got)


def back_kernel(n_sec, count, last, flags_ref, *refs):
    grads, weight_refs, refs = refs[:count], refs[count : count + 3], refs[count + 3 :]
    sec, decoder = flags_ref[0], flags_ref[1]
    tokens = grads[0].shape[1]
    left = [jnp.concatenate([g[i] for g in grads], axis=0) if count > 1 else grads[0][i] for i in range(3)]
    query = product(left[0], weight_refs[0][...], ((1,), (1,)))
    source = product(left[1], weight_refs[1][...], ((1,), (1,)))
    source = source + product(left[2], weight_refs[2][...], ((1,), (1,)))
    stream = query + jnp.where(decoder == 1, 0.0, source)
    memory = jnp.where(decoder == 1, source, 0.0)
    if not last:
        stream_ref, memory_ref = refs
        stream_ref[...] = stream.reshape(stream_ref.shape)
        memory_ref[...] = memory.reshape(memory_ref.shape)
        return
    acc_s, acc_m = refs[:2]
    part_refs, refs = refs[2 : 2 + PARTS * count], refs[2 + PARTS * count :]
    memory_refs, scratch = refs[:-1], refs[-1]
    part, piece = tokens // PARTS, tokens // n_sec
    for p in range(count):
        here = stream[p * tokens : (p + 1) * tokens] + acc_s[p, 0]
        for i in range(PARTS):
            part_refs[p * PARTS + i][...] = here[i * part : (i + 1) * part].astype(BF16)
        scratch[...] = memory[p * tokens : (p + 1) * tokens] + acc_m[p, 0]
        for i, ref in enumerate(memory_refs):
            first = pl.multiple_of(lax.rem(sec + i, n_sec) * piece, piece)
            ref[p] = scratch[pl.ds(first, piece)].astype(ref.dtype)


def back(c, width, weights, grads, flags, n_sec, acc=None, odd=0):
    tokens, rows, places = grads[0].shape[1], weights[0].shape[0], len(grads)
    piece = (places, tokens // n_sec, rows)
    specs = [SMEM] + [full(g) for g in grads] + [columns_of(w, width, c) for w in weights]
    args = (flags, *grads, *weights)
    if acc is None:
        outs = (shaped((places // 2, 2, tokens, rows), F32),) * 2
        scratch = []
    else:
        outs = (shaped((tokens // PARTS, rows), BF16),) * (PARTS * places)
        outs += (shaped(piece, F32),) + (shaped(piece, BF16),) * (n_sec - 1)
        specs += [pl.BlockSpec((places, 1, tokens, rows), lambda i: (0, odd, 0, 0))] * 2
        args += tuple(acc)
        scratch = [pltpu.VMEM((tokens, rows), F32)]
    return pl.pallas_call(
        functools.partial(back_kernel, n_sec, places, acc is not None),
        grid=(1,),
        in_specs=specs,
        out_specs=tuple(full(o) for o in outs),
        out_shape=outs,
        scratch_shapes=scratch,
        compiler_params=pltpu.CompilerParams(vmem_limit_bytes=24 * MIB),
        cost_estimate=cost(3 * places * tokens * rows * width),
        name="back",
    )(*args)


def pick_kernel(share, table_ref, *refs):
    count = table_ref.shape[0]
    blocks, outs = refs[:-count], refs[-count:]
    for q, out_ref in enumerate(outs):
        lanes = pl.ds(pl.multiple_of(table_ref[q, 1] * share, share), share)
        for e, block in enumerate(blocks):

            @pl.when(table_ref[q, 0] == e)
            def _():
                out_ref[...] = block[:, lanes]


def pick(table, blocks, share):
    outs = (shaped((blocks[0].shape[0], share), BF16),) * table.shape[0]
    return pl.pallas_call(
        functools.partial(pick_kernel, share),
        grid=(1,),
        in_specs=[SMEM] + [full(b) for b in blocks],
        out_specs=tuple(full(o) for o in outs),
        out_shape=outs,
        compiler_params=pltpu.CompilerParams(vmem_limit_bytes=8 * MIB),
        cost_estimate=pl.CostEstimate(flops=0, bytes_accessed=4 * len(blocks) * blocks[0].size, transcendentals=0),
        name="pick",
    )(table, *blocks)


def swap(array, axis, size, bit):
    return lax.ppermute(array, axis, [(i, i ^ bit) for i in range(size)])


def shift(array, by):
    size = lax.axis_size("section")
    return lax.ppermute(array, "section", [(s, (s + by) % size) for s in range(size)])


def sum_over(array, axis):
    size, bit = lax.axis_size(axis), 1
    while bit < size:
        array = array + swap(array, axis, size, bit)
        bit *= 2
    return array


def reversed_bits(index, size):
    result, bit = 0, 1
    while bit < size:
        result = result * 2 + (1 if index & bit else 0)
        bit *= 2
    return result


def shards(
    stream, memory_hidden, layer_gain, final_gain, query_weight, key_weight, value_weight,
    cotangent, encoder_lengths, decoder_lengths, assignment,
):
    n_sec, n_tp, n_dp = (lax.axis_size(a) for a in ("section", "tp", "dp"))
    sec, tp, dp = (lax.axis_index(a) for a in ("section", "tp", "dp"))
    decoder = sec >= n_sec // 2
    local = stream[0]
    micro, span, share = local.shape
    slots = memory_hidden.shape[1]
    hidden = share * n_tp
    columns = query_weight.shape[2]
    tokens, mem_tokens = micro * span, micro * slots
    per_row = n_tp // n_dp
    half = n_dp // 2
    width = columns // CHUNKS
    weights = [w[0] for w in (query_weight, key_weight, value_weight)]

    def to_rows(x):
        return x.reshape(micro, n_sec, slots, -1).transpose(1, 0, 2, 3).reshape(tokens, -1)

    def to_samples(x):
        return x.reshape(n_sec, micro, slots, -1).transpose(1, 0, 2, 3).reshape(micro, span, -1)

    layer_share = lax.dynamic_slice_in_dim(layer_gain[0], tp * share, share)
    final_share = lax.dynamic_slice_in_dim(final_gain, tp * share, share)
    stream_f = local.astype(F32)
    memory_f = memory_hidden.astype(F32)
    stream_block = to_rows((stream_f * layer_share).astype(BF16))
    memory_block = (memory_f * final_share).astype(BF16).reshape(mem_tokens, share)

    inward = []
    for j in range(n_tp):
        pairs = []
        for z in range(n_tp):
            for r in range(n_dp):
                to = ((z % per_row) * n_dp + r + j) % n_tp
                pairs.append((z * n_dp + r, to * n_dp + z // per_row))
        inward.append(pairs)
    with jax.named_scope("in_memory"):
        mem_own = jnp.stack([lax.ppermute(memory_block, ("tp", "dp"), pairs) for pairs in inward])
    with jax.named_scope("in_stream"):
        arrived = [lax.ppermute(stream_block, ("tp", "dp"), pairs) for pairs in inward]
    with jax.named_scope("x_memory"):
        memory = [mem_own] + [shift(mem_own, i) for i in range(1, n_sec)]
    place_of = [reversed_bits(p, n_dp) for p in range(n_dp)]

    def table(rows):
        values = np.array([[rows(z, r) for r in range(n_dp)] for z in range(n_tp)], np.int32)
        return lax.dynamic_slice(jnp.array(values), (tp, dp) + (0,) * (values.ndim - 2), (1, 1) + values.shape[2:])[0, 0]

    flags = jnp.stack([sec, decoder.astype(jnp.int32)]).astype(jnp.int32)

    def arrivals(z, r):
        units = [(z - j) % n_tp for j in range(n_tp)]
        return [place_of[(u % n_dp) ^ r] for u in units] + [u // n_dp for u in units]

    where = jnp.concatenate([table(arrivals), flags])

    squares = jnp.concatenate(
        [
            jnp.sum(stream_f * stream_f, axis=2).reshape(micro, n_sec, slots).transpose(1, 0, 2).reshape(tokens),
            jnp.sum(memory_f * memory_f, axis=2).reshape(mem_tokens),
        ]
    )
    inverses = lax.rsqrt(sum_over(squares, "tp") / hidden + EPSILON)
    inverse, mem_inverse = inverses[:tokens], inverses[tokens:]
    scales = [mem_inverse] + [shift(mem_inverse, i) for i in range(1, n_sec)]
    mem_scale = [
        sum(jnp.where((sec - i) % n_sec == h, scales[i], 0.0) for i in range(n_sec)) for h in range(n_sec)
    ]
    scale_q = inverse[:, None]
    scale_s = jnp.where(decoder, jnp.concatenate(mem_scale), inverse)[:, None]

    micros = jnp.arange(micro, dtype=jnp.int32)
    reads = jnp.where(decoder, assignment[0], micros)
    query_len = jnp.where(decoder, decoder_lengths, encoder_lengths)
    index = jnp.arange(tokens, dtype=jnp.int32)
    sample = (index // slots) % micro
    position = (index // (micro * slots)) * slots + index % slots

    def of_sample(values):
        return sum(jnp.where(sample == m, values[m], 0) for m in range(micro))

    opened = (of_sample(reads)[:, None] == sample[None, :]) & (position < of_sample(encoder_lengths))[None, :]
    opened = opened.astype(F32)
    live = (position < of_sample(query_len)).astype(F32)[:, None]
    raw = to_rows(cotangent[0])

    mixes, grads, dot_q, dot_s = [], [], 0.0, 0.0
    x = s = acc = None
    for c in range(CHUNKS):
        if c == 0:
            x, s, keep, send = project(c, width, weights, n_dp, n_sec, where, arrived, memory)
        else:
            x, s, keep, send = project(c, width, weights, n_dp, n_sec, where, x=x, s=s)
        bit = 1
        while True:
            with jax.named_scope(f"reduce_{bit}_{c}"):
                got = swap(send, "dp", n_dp, bit)
            bit *= 2
            if bit == n_dp:
                break
            keep, send = combine(keep, got)
        with jax.named_scope(f"attention_{c}"):
            mix, grad, piece_q, piece_s = attention(
                keep, got, raw, scale_q, scale_s, opened, live, c
            )
        mixes.append(mix)
        dot_q, dot_s = dot_q + piece_q, dot_s + piece_s
        held = [grad]
        while bit > 1:
            bit //= 2
            with jax.named_scope(f"gather_{bit}_{c}"):
                held = held + [swap(h, "dp", n_dp, bit) for h in held]
        grads.append(held)
        if c < CHUNKS - 1:
            new = back(c, width, weights, held, flags, n_sec)
            acc = new if acc is None else (acc[0] + new[0], acc[1] + new[1])

    row_q, row_s = jnp.sum(dot_q, axis=1), jnp.sum(dot_s, axis=1)
    row_stream = row_q + jnp.where(decoder, 0.0, row_s)
    row_memory = jnp.where(decoder, row_s, 0.0).reshape(n_sec, mem_tokens)
    mem_rows = lax.dynamic_slice_in_dim(row_memory, sec, 1, 0)
    for i in range(1, n_sec):
        mem_rows = mem_rows + shift(lax.dynamic_slice_in_dim(row_memory, (sec + i) % n_sec, 1, 0), i)
    row_dots = sum_over(jnp.concatenate([row_stream, mem_rows.reshape(mem_tokens)]), "tp") / hidden

    last = CHUNKS - 1
    blocks = [[None] * n_dp for _ in range(PARTS + 1)]
    for odd in (1, 0):
        with jax.named_scope(f"back_{odd}"):
            got = back(last, width, weights, grads[last][odd::2], flags, n_sec, acc, odd)
        parts, held, sent = got[: PARTS * half], got[PARTS * half], got[PARTS * half + 1 :]
        with jax.named_scope(f"x_back_{odd}"):
            others = [shift(a, i + 1) for i, a in enumerate(sent)]
        for p in range(half):
            for i in range(PARTS):
                blocks[i][2 * p + odd] = parts[p * PARTS + i]
            total = held[p]
            for a in others:
                total = total + a[p].astype(F32)
            blocks[PARTS][2 * p + odd] = total.astype(BF16)

    def picks(z, r):
        return [[((q ^ z) // per_row) ^ r, (q ^ z) % per_row] for q in range(n_tp)]

    picked = table(picks)
    totals = []
    for part, leaving in enumerate(blocks):
        here = [leaving[0]]
        for e in range(1, n_dp):
            with jax.named_scope(f"turn_{part}_{e}"):
                here.append(swap(leaving[place_of[e]], "dp", n_dp, e))
        sums = dict(enumerate(pick(picked, here, share)))
        bit = 1
        while bit < n_tp:
            for q in sorted((q for q in sums if q & bit), reverse=True):
                with jax.named_scope(f"out_{part}_{bit}_{q}"):
                    got = swap(sums.pop(q).astype(BF16), "tp", n_tp, bit)
                sums[q ^ bit] = sums[q ^ bit].astype(F32) + got.astype(F32)
            bit *= 2
        totals.append(sums[0])
    total = to_samples(jnp.concatenate(totals[:PARTS], axis=0))
    factor = to_samples(inverse * inverse * row_dots[:tokens])
    stream_out = layer_share * total - stream_f * factor
    mem_factor = (mem_inverse * mem_inverse * row_dots[tokens:]).reshape(micro, slots, 1)
    memory_out = final_share * totals[PARTS].reshape(micro, slots, share) - memory_f * mem_factor

    def weight_grad(left, i):
        rows = [jnp.concatenate([grads[c][p][i] for c in range(CHUNKS)], axis=-1) for p in range(n_dp)]
        return dot(
            left.reshape(n_dp * tokens, -1), jnp.concatenate(rows, axis=0), ((0,), (0,))
        ).astype(BF16)[None]

    return (
        to_samples(jnp.concatenate(mixes, axis=-1))[None],
        stream_out.astype(BF16)[None],
        memory_out.astype(BF16),
        weight_grad(x, 0),
        weight_grad(s, 1),
        weight_grad(s, 2),
    )


def solution(mesh):
    placed = (
        P("section", "dp", None, "tp"),
        P("dp", "section", "tp"),
        P("section", None),
        P(),
        P("section", "dp", "tp"),
        P("section", "dp", "tp"),
        P("section", "dp", "tp"),
        P("section", "dp", None, "tp"),
        P("dp"),
        P("dp"),
        P("dp", None),
    )
    return jax.shard_map(
        shards,
        mesh=mesh,
        in_specs=placed,
        out_specs=(
            P("section", "dp", None, "tp"),
            P("section", "dp", None, "tp"),
            P("dp", "section", "tp"),
            P("section", "dp", "tp"),
            P("section", "dp", "tp"),
            P("section", "dp", "tp"),
        ),
        check_vma=False,
    )
```
